32 devices in a mesh: shard: 4 (over x, core), ctx: 4 (over z), tp: 2 (over y).
Axes of the slice: x: 2, y: 2, z: 4, core: 2. Of those that a mesh axis runs over, the one named last changes fastest.
Arguments:
- block_input: bfloat16 [4, 4096, 2048], P('shard', 'ctx', 'tp'), may hold values from -6 to 6
- out_cotangent: bfloat16 [4, 4096, 2048], P('shard', 'ctx', 'tp'), may hold values from -8 to 8
- segment_ids: int32 [4, 4096], P('shard'), may hold values from 0 to 3, never falling along the last dimension, each value on 1 to 2048 neighbouring positions
- qkv_weight: float32 [2048, 8, 768], P('shard', 'tp'), may hold values from -0.125 to 0.125
- qkv_weight_first: float32 [2048, 8, 768], P('shard', 'tp'), may hold values from -48 to 48
- qkv_weight_second: float32 [2048, 8, 768], P('shard', 'tp'), may hold values from 64 to 1024
- dense_weight: float32 [2048, 2048], P('shard', 'tp'), may hold values from -0.5 to 0.5
- dense_weight_first: float32 [2048, 2048], P('shard', 'tp'), may hold values from -48 to 48
- dense_weight_second: float32 [2048, 2048], P('shard', 'tp'), may hold values from 64 to 1024
- widen_weight: float32 [2048, 8192], P('shard', 'tp'), may hold values from -0.125 to 0.125
- widen_weight_first: float32 [2048, 8192], P('shard', 'tp'), may hold values from -48 to 48
- widen_weight_second: float32 [2048, 8192], P('shard', 'tp'), may hold values from 64 to 1024
- narrow_weight: float32 [2048, 8192], P('shard', 'tp'), may hold values from -0.0625 to 0.0625
- narrow_weight_first: float32 [2048, 8192], P('shard', 'tp'), may hold values from -48 to 48
- narrow_weight_second: float32 [2048, 8192], P('shard', 'tp'), may hold values from 64 to 1024
- attn_bias: float32 [8, 768], replicated, may hold values from -1.75 to 1.75
- attn_bias_first: float32 [8, 768], replicated, may hold values from -48 to 48
- attn_bias_second: float32 [8, 768], replicated, may hold values from 64 to 1024
- hidden_bias: float32 [8192], replicated, may hold values from -1.75 to 1.75
- hidden_bias_first: float32 [8192], replicated, may hold values from -48 to 48
- hidden_bias_second: float32 [8192], replicated, may hold values from 64 to 1024
- out_bias: float32 [2, 2048], replicated, may hold values from -1.75 to 1.75
- out_bias_first: float32 [2, 2048], replicated, may hold values from -48 to 48
- out_bias_second: float32 [2, 2048], replicated, may hold values from 64 to 1024
- norm_gains: float32 [2, 2048], replicated, may hold values from 0.1 to 1.9
- norm_gains_first: float32 [2, 2048], replicated, may hold values from -48 to 48
- norm_gains_second: float32 [2, 2048], replicated, may hold values from 64 to 1024
- norm_shifts: float32 [2, 2048], replicated, may hold values from -1.75 to 1.75
- norm_shifts_first: float32 [2, 2048], replicated, may hold values from -48 to 48
- norm_shifts_second: float32 [2, 2048], replicated, may hold values from 64 to 1024
Outputs:
- block_out: bfloat16 [4, 4096, 2048], P('shard', 'ctx', 'tp')
- input_grad: bfloat16 [4, 4096, 2048], P('shard', 'ctx', 'tp')
- qkv_weight_grad: float32 [2048, 8, 768], P('shard', 'tp')
- qkv_weight_new: float32 [2048, 8, 768], P('shard', 'tp')
- qkv_weight_first_new: float32 [2048, 8, 768], P('shard', 'tp')
- qkv_weight_second_new: float32 [2048, 8, 768], P('shard', 'tp')
- dense_weight_grad: float32 [2048, 2048], P('shard', 'tp')
- dense_weight_new: float32 [2048, 2048], P('shard', 'tp')
- dense_weight_first_new: float32 [2048, 2048], P('shard', 'tp')
- dense_weight_second_new: float32 [2048, 2048], P('shard', 'tp')
- widen_weight_grad: float32 [2048, 8192], P('shard', 'tp')
- widen_weight_new: float32 [2048, 8192], P('shard', 'tp')
- widen_weight_first_new: float32 [2048, 8192], P('shard', 'tp')
- widen_weight_second_new: float32 [2048, 8192], P('shard', 'tp')
- narrow_weight_grad: float32 [2048, 8192], P('shard', 'tp')
- narrow_weight_new: float32 [2048, 8192], P('shard', 'tp')
- narrow_weight_first_new: float32 [2048, 8192], P('shard', 'tp')
- narrow_weight_second_new: float32 [2048, 8192], P('shard', 'tp')
- attn_bias_grad: float32 [8, 768], replicated
- attn_bias_new: float32 [8, 768], replicated
- attn_bias_first_new: float32 [8, 768], replicated
- attn_bias_second_new: float32 [8, 768], replicated
- hidden_bias_grad: float32 [8192], replicated
- hidden_bias_new: float32 [8192], replicated
- hidden_bias_first_new: float32 [8192], replicated
- hidden_bias_second_new: float32 [8192], replicated
- out_bias_grad: float32 [2, 2048], replicated
- out_bias_new: float32 [2, 2048], replicated
- out_bias_first_new: float32 [2, 2048], replicated
- out_bias_second_new: float32 [2, 2048], replicated
- norm_gains_grad: float32 [2, 2048], replicated
- norm_gains_new: float32 [2, 2048], replicated
- norm_gains_first_new: float32 [2, 2048], replicated
- norm_gains_second_new: float32 [2, 2048], replicated
- norm_shifts_grad: float32 [2, 2048], replicated
- norm_shifts_new: float32 [2, 2048], replicated
- norm_shifts_first_new: float32 [2, 2048], replicated
- norm_shifts_second_new: float32 [2, 2048], replicated
The draws below stay inside these ranges and needn't reach their ends.
Inputs may be any that keep to these rules, and one draw needn't show every extreme that they name: `segment_ids`: within a sequence the segment ids never fall; each of the 4 ids covers 1 to 2048 consecutive tokens, and some id covers exactly 2048.
All inputs are finite; a program needn't handle non-finite values.
Results may differ from the reference program's by a relative error of at most 0.0055.
The reference program's roundings to bfloat16 on the way count: a program that leaves them out, or rounds other values in their place, can miss the bound.
Values may be sent and summed in bfloat16 or wider, within the bound.
No kernel may reach another device: no remote copies, remote signals or barrier semaphores. Data moves between devices by JAX's collectives and lax.ppermute only.
A program may use at most 704 MiB of HBM per device.

```python
import math
import jax
import jax.numpy as jnp
import numpy as np
from jax import lax

D = 2048
H = 8
HD = 256
ROT = 64
FF = 8192
DOCS = 4
STEP = 4
LEN = 4096
SEQS = 4
TOKENS = 16384
DOC_MOST = 2048


def strengthened(entries, key, source, target, parts, factor):
    def block_of(dim):
        return (jnp.arange(entries.shape[dim]) // (entries.shape[dim] // parts)).reshape((-1,) + (1,) * (entries.ndim - 1 - dim))

    one_side = jax.random.permutation(key, parts)[block_of(target)]
    far = (block_of(target) + parts // 2) % parts
    return jnp.where((block_of(source) == one_side) | (block_of(source) == far), factor * entries, entries)


def levels(own_key, dims, shards, smallest, top_value):
    level = 1.0
    for dim, parts in shards:
        draws = jax.random.uniform(jax.random.fold_in(jax.random.fold_in(own_key, 6), dim), (parts,), jnp.float32, smallest / len(shards), top_value / len(shards))
        level = level * jnp.repeat(jnp.exp(draws), dims[dim] // parts).reshape((-1,) + (1,) * (len(dims) - 1 - dim))
    return level


def profile(count, total, reach, lean):
    weights = [(1 << 20) // math.isqrt(standing ** lean) + 1 for standing in range(2, count + 1)]
    rest, holding = total - reach - (count - 1), [1] * (count - 1)
    while rest > 0:
        candidates = [i for i in range(count - 1) if holding[i] < reach]
        whole, remaining = sum([weights[i] for i in candidates]), rest
        for i in candidates:
            addition = min(reach - holding[i], max(1, remaining * weights[i] // whole), rest)
            holding[i] = holding[i] + addition
            rest = rest - addition
    return np.array([reach] + holding)


def ragged_sizes(rng, number_of, total, limit, lean):
    if number_of == 2:
        one = jax.random.randint(rng, (), max(1, total - limit), min(limit, total - 1) + 1)
        return jnp.stack([one, total - one])
    sizes = jnp.asarray(profile(number_of, total, limit, lean), jnp.int32)
    couples = (number_of - 1) // 2
    giver, sink = sizes[1:1 + 2 * couples:2], sizes[2:2 + 2 * couples:2]
    margin = jnp.minimum(giver - 1, limit - sink)
    shifted = jax.random.randint(jax.random.fold_in(rng, 1), (couples,), 0, 1 << 20) % (margin + 1)
    sizes = sizes.at[1:1 + 2 * couples:2].set(giver - shifted).at[2:2 + 2 * couples:2].set(sink + shifted)
    return sizes[jax.random.permutation(jax.random.fold_in(rng, 2), number_of)]


def scatter_about(key, extent, spread, most, split=(), held_as=jnp.bfloat16):
    entries = jax.random.normal(key, extent, jnp.float32) * spread
    if len(split) > 0:
        entries = levels(key, extent, split, -0.22, 0.18) * entries
    return jnp.clip(entries, min=-most, max=most).astype(held_as)


def gaussian_with(rng, dims, width, reach, shards, heavy, kind=jnp.bfloat16):
    result = width * jax.random.normal(rng, dims, jnp.float32)
    if shards:
        result = result * levels(rng, dims, shards, -0.22, 0.18)
    return jnp.clip(strengthened(result, jax.random.fold_in(rng, 3), *heavy), -reach, reach).astype(kind)


def setup_inputs(seed: int = 0) -> dict:
    splits = jax.random.split(jax.random.key(seed), 31)
    return {
        "block_input": scatter_about(splits[0], (SEQS, LEN, D), 1.0, 6.0, ((0, 4), (1, 4), (2, 2))),
        "out_cotangent": gaussian_with(splits[1], (SEQS, LEN, D), 1.0, 8.0, ((0, 4), (1, 4), (2, 2)), (1, 2, 4, 2.0)),
        "segment_ids": jax.vmap(lambda own: jnp.searchsorted(jnp.cumsum(ragged_sizes(own, DOCS, LEN, DOC_MOST, 1)), jnp.arange(LEN), side="right"))(jax.random.split(splits[2], SEQS)).reshape((SEQS, LEN)).astype(jnp.int32),
        "qkv_weight": scatter_about(splits[3], (D, H, 3 * HD), D ** -0.5, 0.125, ((0, 4), (1, 2)), jnp.float32),
        "qkv_weight_first": scatter_about(splits[4], (D, H, 3 * HD), (max(TOKENS // 2048, 1)), 48.0, ((0, 4), (1, 2)), jnp.float32),
        "qkv_weight_second": jnp.clip(jnp.exp(math.log(1024.0) - 2.7725887 * jax.random.uniform(splits[5], (D, H, 3 * HD), jnp.float32) ** levels(splits[5], (D, H, 3 * HD), ((0, 4), (1, 2)), -0.2, 0.2)), 64.0, 1024.0),
        "dense_weight": scatter_about(splits[6], (D, H * HD), (H * HD // 16) ** -0.5, 0.5, ((0, 4), (1, 2)), jnp.float32),
        "dense_weight_first": scatter_about(splits[7], (D, H * HD), (max(TOKENS // 2048, 1)), 48.0, ((0, 4), (1, 2)), jnp.float32),
        "dense_weight_second": jnp.clip(jnp.exp(math.log(1024.0) - 2.7725887 * jax.random.uniform(splits[8], (D, H * HD), jnp.float32) ** levels(splits[8], (D, H * HD), ((0, 4), (1, 2)), -0.2, 0.2)), 64.0, 1024.0),
        "widen_weight": scatter_about(splits[9], (D, FF), D ** -0.5, 0.125, ((0, 4), (1, 2)), jnp.float32),
        "widen_weight_first": scatter_about(splits[10], (D, FF), (max(TOKENS // 2048, 1)), 48.0, ((0, 4), (1, 2)), jnp.float32),
        "widen_weight_second": jnp.clip(jnp.exp(math.log(1024.0) - 2.7725887 * jax.random.uniform(splits[11], (D, FF), jnp.float32) ** levels(splits[11], (D, FF), ((0, 4), (1, 2)), -0.2, 0.2)), 64.0, 1024.0),
        "narrow_weight": scatter_about(splits[12], (D, FF), FF ** -0.5, 0.0625, ((0, 4), (1, 2)), jnp.float32),
        "narrow_weight_first": scatter_about(splits[13], (D, FF), (max(TOKENS // 2048, 1)), 48.0, ((0, 4), (1, 2)), jnp.float32),
        "narrow_weight_second": jnp.clip(jnp.exp(math.log(1024.0) - 2.7725887 * jax.random.uniform(splits[14], (D, FF), jnp.float32) ** levels(splits[14], (D, FF), ((0, 4), (1, 2)), -0.2, 0.2)), 64.0, 1024.0),
        "attn_bias": scatter_about(splits[15], (H, 3 * HD), 0.3, 1.75, (), jnp.float32),
        "attn_bias_first": scatter_about(splits[16], (H, 3 * HD), (max(TOKENS // 2048, 1)), 48.0, (), jnp.float32),
        "attn_bias_second": jnp.clip(jnp.exp(jax.random.uniform(splits[17], (H, 3 * HD), jnp.float32, math.log(64.0), math.log(1024.0))), 64.0, 1024.0),
        "hidden_bias": scatter_about(splits[18], (FF,), 0.3, 1.75, (), jnp.float32),
        "hidden_bias_first": scatter_about(splits[19], (FF,), (max(TOKENS // 2048, 1)), 48.0, (), jnp.float32),
        "hidden_bias_second": jnp.clip(jnp.exp(jax.random.uniform(splits[20], (FF,), jnp.float32, math.log(64.0), math.log(1024.0))), 64.0, 1024.0),
        "out_bias": scatter_about(splits[21], (2, D), 0.3, 1.75, (), jnp.float32),
        "out_bias_first": scatter_about(splits[22], (2, D), (max(TOKENS // 2048, 1)), 48.0, (), jnp.float32),
        "out_bias_second": jnp.clip(jnp.exp(jax.random.uniform(splits[23], (2, D), jnp.float32, math.log(64.0), math.log(1024.0))), 64.0, 1024.0),
        "norm_gains": jnp.clip(1.0 + 0.18 * jax.random.normal(splits[24], (2, D), jnp.float32), 0.1, 1.9),
        "norm_gains_first": scatter_about(splits[25], (2, D), (max(TOKENS // 2048, 1)), 48.0, (), jnp.float32),
        "norm_gains_second": jnp.clip(jnp.exp(jax.random.uniform(splits[26], (2, D), jnp.float32, math.log(64.0), math.log(1024.0))), 64.0, 1024.0),
        "norm_shifts": scatter_about(splits[27], (2, D), 0.3, 1.75, (), jnp.float32),
        "norm_shifts_first": scatter_about(splits[28], (2, D), (max(TOKENS // 2048, 1)), 48.0, (), jnp.float32),
        "norm_shifts_second": jnp.clip(jnp.exp(jax.random.uniform(splits[29], (2, D), jnp.float32, math.log(64.0), math.log(1024.0))), 64.0, 1024.0),
    }


@jax.custom_vjp
def low(v):
    return lax.optimization_barrier(v.astype(jnp.bfloat16)).astype(jnp.float32)

@jax.custom_vjp
def low_back(v):
    return v

def low_keep(v):
    return (low(v), None)

def low_pass(kept, grad):
    return (grad,)

def back_keep(v):
    return (v, None)

def back_low(kept, grad):
    return (low(grad),)
low.defvjp(low_keep, low_pass)
low_back.defvjp(back_keep, back_low)
highest = lax.Precision.HIGHEST
beta_one = 0.9
beta_two = 0.95
matrix_rate = 0.01
vector_rate = 0.05
decay_rate = 0.01
adam_eps = 1e-08
norm_eps = 1e-05

def rotate_heads(values, cos_table, sin_table, rot_width):
    half_rot = rot_width // 2
    head_part = values[..., :rot_width]
    turned = jnp.concatenate([-head_part[..., half_rot:], head_part[..., :half_rot]], -1)
    return jnp.concatenate([head_part * cos_table + turned * sin_table, values[..., rot_width:]], -1)

def adam_step(weight, gradient, first_moment, second_moment, step_rate, weight_decay):
    first_new = beta_one * first_moment + (1.0 - beta_one) * gradient
    second_new = beta_two * second_moment + (1.0 - beta_two) * gradient * gradient
    first_hat = first_new / (1.0 - beta_one ** STEP)
    second_hat = second_new / (1.0 - beta_two ** STEP)
    weight_new = weight - step_rate * (first_hat / (jnp.sqrt(second_hat) + adam_eps) + weight_decay * weight)
    return (weight_new, first_new, second_new)

def layer_one(param_set, inputs, seq_segs):
    qkv_mat, dense_mat, widen_mat, narrow_mat, attn_shift, hidden_shift, out_shift, gain_rows, shift_rows = param_set
    token_index = jnp.arange(LEN, dtype=jnp.int32)
    before = lax.optimization_barrier(jnp.sum((seq_segs[None, :] < seq_segs[:, None]).astype(jnp.int32), axis=1)).astype(jnp.int32)
    positions = (token_index - before).astype(jnp.float32)
    inv_freq = 10000.0 ** (-2.0 * jnp.arange(ROT // 2, dtype=jnp.float32) / ROT)
    angles = positions[:, None, None] * inv_freq
    cos_table = jnp.concatenate([jnp.cos(angles), jnp.cos(angles)], -1)
    sin_table = jnp.concatenate([jnp.sin(angles), jnp.sin(angles)], -1)
    allowed = (seq_segs[:, None] == seq_segs[None, :]) & (token_index[None, :] <= token_index[:, None])
    row_mean = lax.optimization_barrier(jnp.mean(inputs, axis=-1, keepdims=True))
    centered = inputs - row_mean
    row_var = lax.optimization_barrier(jnp.mean(centered * centered, axis=-1, keepdims=True))
    normed = centered * lax.rsqrt(row_var + norm_eps)
    first_in = low(normed * gain_rows[0] + shift_rows[0])
    second_in = low(normed * gain_rows[1] + shift_rows[1])
    projected = jnp.dot(first_in, low(qkv_mat).reshape(D, H * 3 * HD), precision=highest).reshape(LEN, H, 3 * HD)
    projected = low_back(projected + attn_shift)
    query_low = low(rotate_heads(projected[..., :HD], cos_table, sin_table, ROT))
    key_low = low(rotate_heads(projected[..., HD:2 * HD], cos_table, sin_table, ROT))
    value_low = low(projected[..., 2 * HD:])
    scores = low_back(jnp.einsum('ihd,jhd->hij', query_low, key_low, precision=highest) * HD ** (-0.5))
    exp_scores = jnp.where(allowed[None], jnp.exp(scores), 0.0)
    attn_probs = exp_scores / lax.optimization_barrier(jnp.sum(exp_scores, axis=-1, keepdims=True))
    probs_low = low(attn_probs)
    attended = jnp.einsum('hij,jhd->ihd', probs_low, value_low, precision=highest)
    attended = low_back(low(attended)).reshape(LEN, H * HD)
    attn_out = jnp.dot(attended, low(dense_mat).T, precision=highest) + out_shift[0]
    widened = low_back(jnp.dot(second_in, low(widen_mat), precision=highest) + hidden_shift)
    activated = low(jax.nn.gelu(widened, approximate=False))
    mlp_out = jnp.dot(activated, low(narrow_mat).T, precision=highest) + out_shift[1]
    return inputs + attn_out + mlp_out

def reference(block_input, out_cotangent, segment_ids, qkv_weight, qkv_weight_first, qkv_weight_second, dense_weight, dense_weight_first, dense_weight_second, widen_weight, widen_weight_first, widen_weight_second, narrow_weight, narrow_weight_first, narrow_weight_second, attn_bias, attn_bias_first, attn_bias_second, hidden_bias, hidden_bias_first, hidden_bias_second, out_bias, out_bias_first, out_bias_second, norm_gains, norm_gains_first, norm_gains_second, norm_shifts, norm_shifts_first, norm_shifts_second):
    params = (qkv_weight, dense_weight, widen_weight, narrow_weight, attn_bias, hidden_bias, out_bias, norm_gains, norm_shifts)
    firsts = (qkv_weight_first, dense_weight_first, widen_weight_first, narrow_weight_first, attn_bias_first, hidden_bias_first, out_bias_first, norm_gains_first, norm_shifts_first)
    seconds = (qkv_weight_second, dense_weight_second, widen_weight_second, narrow_weight_second, attn_bias_second, hidden_bias_second, out_bias_second, norm_gains_second, norm_shifts_second)

    def forward(param_set, inputs):
        layer_fn = jax.checkpoint(layer_one)
        return lax.map(lambda pair: layer_fn(param_set, pair[0], pair[1]), (inputs, segment_ids))
    block_out, pull_back = jax.vjp(forward, params, block_input.astype(jnp.float32))
    all_grads, input_grad = pull_back(out_cotangent.astype(jnp.float32))
    results = [block_out.astype(jnp.bfloat16), input_grad.astype(jnp.bfloat16)]
    for slot in range(9):
        step_rate = matrix_rate if slot < 4 else vector_rate
        weight_decay = decay_rate if slot < 4 else 0.0
        weight_new, first_new, second_new = adam_step(params[slot], all_grads[slot], firsts[slot], seconds[slot], step_rate, weight_decay)
        results.extend([all_grads[slot], weight_new, first_new, second_new])
    return (results[0], results[1], results[2], results[3], results[4], results[5], results[6], results[7], results[8], results[9], results[10], results[11], results[12], results[13], results[14], results[15], results[16], results[17], results[18], results[19], results[20], results[21], results[22], results[23], results[24], results[25], results[26], results[27], results[28], results[29], results[30], results[31], results[32], results[33], results[34], results[35], results[36], results[37])
```

```python
import functools

import jax
import jax.numpy as jnp
from jax import lax
from jax.experimental import pallas as pl
from jax.experimental.pallas import tpu as pltpu
from jax.sharding import PartitionSpec as P

D = 2048
H = 8
HD = 256
ROT = 64
FF = 8192
STEP = 4
DOC_IDS = 4
DOC_MOST = 2048

beta_one = 0.9
beta_two = 0.95
matrix_rate = 0.01
vector_rate = 0.05
decay_rate = 0.01
adam_eps = 1e-08
norm_eps = 1e-05

Q_TILE = 512
K_TILE = 512
F32 = jnp.float32
BF16 = jnp.bfloat16


def rotate_wide(values, cos_table, sin_table, group):
    tokens, width = values.shape
    heads = width // group
    half = ROT // 2
    split = values.reshape(tokens, heads, group)
    part = split[..., :ROT]
    turned = jnp.concatenate([-part[..., half:], part[..., :half]], -1)
    moved = part * cos_table[:, None, :] + turned * sin_table[:, None, :]
    return jnp.concatenate([moved, split[..., ROT:]], -1).reshape(tokens, width)


def adam_step(weight, gradient, first_moment, second_moment, step_rate, weight_decay):
    first_new = beta_one * first_moment + (1.0 - beta_one) * gradient
    second_new = beta_two * second_moment + (1.0 - beta_two) * gradient * gradient
    first_hat = first_new / (1.0 - beta_one**STEP)
    second_hat = second_new / (1.0 - beta_two**STEP)
    weight_new = weight - step_rate * (
        first_hat / (jnp.sqrt(second_hat) + adam_eps) + weight_decay * weight
    )
    return (weight_new, first_new, second_new)


def dot_nn(a, b):
    return lax.dot_general(a, b, (((1,), (0,)), ((), ())), preferred_element_type=F32)


def dot_nt(a, b):
    return lax.dot_general(a, b, (((1,), (1,)), ((), ())), preferred_element_type=F32)


def dot_tn(a, b):
    return lax.dot_general(a, b, (((0,), (0,)), ((), ())), preferred_element_type=F32)


def attention_kernel(
    blocks, low_ref, start_ref, q_ref, grad_ref, *rest
):
    kv_refs = rest[:blocks]
    out_ref, dq_ref = rest[blocks : blocks + 2]
    dkv_refs = rest[blocks + 2 : 2 * blocks + 2]
    k_all, v_all, dk_all, dv_all, exps, dprobs = rest[2 * blocks + 2 :]
    tile = pl.program_id(1)
    local = kv_refs[0].shape[0]
    own = (blocks - 1) * local

    @pl.when(tile == 0)
    def _():
        for b in range(blocks):
            k_all[b * local : (b + 1) * local, :] = kv_refs[b][:, :HD]
            v_all[b * local : (b + 1) * local, :] = kv_refs[b][:, HD:]
        dk_all[...] = jnp.zeros_like(dk_all)
        dv_all[...] = jnp.zeros_like(dv_all)

    q = q_ref[...]
    grad = grad_ref[...]
    starts = start_ref[...]
    rows = own + tile * Q_TILE + lax.broadcasted_iota(jnp.int32, (1, Q_TILE), 1)
    first = low_ref[tile]
    last = (own + (tile + 1) * Q_TILE + K_TILE - 1) // K_TILE

    def gather(step, carry):
        total, mixed = carry
        at = pl.multiple_of(step * K_TILE, K_TILE)
        scores = dot_nt(k_all[pl.ds(at, K_TILE), :], q)
        keys = at + lax.broadcasted_iota(jnp.int32, (K_TILE, 1), 0)
        allowed = (keys >= starts) & (keys <= rows)
        exp_scores = jnp.where(allowed, jnp.exp(scores), 0.0)
        dprob = dot_nt(v_all[pl.ds(at, K_TILE), :], grad)
        exps[pl.ds(at, K_TILE), :] = exp_scores
        dprobs[pl.ds(at, K_TILE), :] = dprob
        total = total + jnp.sum(exp_scores, axis=0, keepdims=True)
        mixed = mixed + jnp.sum(exp_scores * dprob, axis=0, keepdims=True)
        return total, mixed

    zero = jnp.zeros((1, Q_TILE), F32)
    total, mixed = lax.fori_loop(first, last, gather, (zero, zero))
    inverse = 1.0 / total
    mean = mixed * inverse
    out_ref[...] = jnp.zeros_like(out_ref)

    def spread(step, carry):
        out, dq = carry
        at = pl.multiple_of(step * K_TILE, K_TILE)
        keys = k_all[pl.ds(at, K_TILE), :]
        values = v_all[pl.ds(at, K_TILE), :]
        probs = exps[pl.ds(at, K_TILE), :] * inverse
        probs_low = probs.astype(BF16)
        dscore = (probs * (dprobs[pl.ds(at, K_TILE), :] - mean)).astype(BF16)
        out = out + dot_tn(probs_low, values)
        dq = dq + dot_tn(dscore, keys)
        dv_all[pl.ds(at, K_TILE), :] += dot_nn(probs_low, grad)
        dk_all[pl.ds(at, K_TILE), :] += dot_nn(dscore, q)
        return out, dq

    blank = jnp.zeros((Q_TILE, HD), F32)
    out, dq = lax.fori_loop(first, last, spread, (blank, blank))
    out_ref[...] = out.astype(BF16)
    dq_ref[...] = dq * (HD ** (-0.5))

    @pl.when(tile == pl.num_programs(1) - 1)
    def _():
        for b in range(blocks):
            kind = dkv_refs[b].dtype
            dkv_refs[b][:, :HD] = dk_all[b * local : (b + 1) * local, :].astype(kind)
            dkv_refs[b][:, HD:] = dv_all[b * local : (b + 1) * local, :].astype(kind)


def attention(q, grad, windows, starts, low):
    tokens, width = q.shape
    heads = width // HD
    blocks = len(windows)
    total = blocks * tokens
    tiles = tokens // Q_TILE
    kinds = [BF16] + [F32] * (blocks - 1) if blocks > 1 else [F32]
    block = lambda: pl.BlockSpec((tokens, 2 * HD), lambda h, i, low: (0, h))
    part = lambda: pl.BlockSpec((Q_TILE, HD), lambda h, i, low: (i, h))
    return pl.pallas_call(
        functools.partial(attention_kernel, blocks),
        out_shape=[
            jax.ShapeDtypeStruct((tokens, width), BF16),
            jax.ShapeDtypeStruct((tokens, width), F32),
        ]
        + [jax.ShapeDtypeStruct((tokens, 2 * width), kind) for kind in kinds],
        grid_spec=pltpu.PrefetchScalarGridSpec(
            num_scalar_prefetch=1,
            grid=(heads, tiles),
            in_specs=[pl.BlockSpec((1, Q_TILE), lambda h, i, low: (0, i)), part(), part()]
            + [block() for _ in windows],
            out_specs=[part(), part()] + [block() for _ in windows],
            scratch_shapes=[
                pltpu.VMEM((total, HD), BF16),
                pltpu.VMEM((total, HD), BF16),
                pltpu.VMEM((total, HD), F32),
                pltpu.VMEM((total, HD), F32),
                pltpu.VMEM((total, Q_TILE), F32),
                pltpu.VMEM((total, Q_TILE), F32),
            ],
        ),
        compiler_params=pltpu.CompilerParams(
            dimension_semantics=("arbitrary", "arbitrary"),
            vmem_limit_bytes=60 * 1024 * 1024,
        ),
        cost_estimate=pl.CostEstimate(
            flops=6 * heads * tokens * total * HD,
            bytes_accessed=12 * tokens * width * blocks,
            transcendentals=heads * tokens * total // 2,
        ),
        name="attention_both_ways",
    )(low, starts, q, grad, *windows)


def swap(values, axis, size, bit):
    return lax.ppermute(values, axis, [(i, i ^ bit) for i in range(size)])


def all_sum(values, axis, size):
    bit = 1
    while bit < size:
        values = values + swap(values, axis, size, bit)
        bit *= 2
    return values


def order_of(bits):
    if not bits:
        return [0]
    rest = order_of(bits[1:])
    return [entry | bits[0] for entry in rest] + rest


def after(values, *others):
    return lax.optimization_barrier((values, *others))[0]


def body(
    sizes,
    block_input,
    out_cotangent,
    segment_ids,
    qkv_weight,
    qkv_weight_first,
    qkv_weight_second,
    dense_weight,
    dense_weight_first,
    dense_weight_second,
    widen_weight,
    widen_weight_first,
    widen_weight_second,
    narrow_weight,
    narrow_weight_first,
    narrow_weight_second,
    attn_bias,
    attn_bias_first,
    attn_bias_second,
    hidden_bias,
    hidden_bias_first,
    hidden_bias_second,
    out_bias,
    out_bias_first,
    out_bias_second,
    norm_gains,
    norm_gains_first,
    norm_gains_second,
    norm_shifts,
    norm_shifts_first,
    norm_shifts_second,
):
    shards, ctxs, tps = sizes["shard"], sizes["ctx"], sizes["tp"]
    _, tokens, width_part = block_input.shape
    full_len = segment_ids.shape[1]
    rows = qkv_weight.shape[0]
    heads = qkv_weight.shape[1]
    hidden = widen_weight.shape[1]
    me = lax.axis_index("shard")
    ctx = lax.axis_index("ctx")
    tp = lax.axis_index("tp")
    bits = [1 << i for i in range(shards.bit_length() - 1)]
    order = order_of(bits)
    chunks = 2 if heads % 2 == 0 else 1
    per = heads // chunks
    back = min(ctxs - 1, (DOC_MOST - 1 + tokens - 1) // tokens)

    place = jnp.asarray([order.index(r) for r in range(shards)], jnp.int32)

    def gather_rows(own):
        held = {0: own}
        for bit in reversed(bits):
            for r in list(held):
                held[r | bit] = swap(held[r], "shard", shards, bit)
        return jnp.concatenate([held[r] for r in order], axis=0)

    def to_near(values, at=lambda piece: piece):
        return jnp.concatenate(
            [
                lax.dynamic_slice_in_dim(values, at(jnp.bitwise_xor(me, r)) * rows, rows, values.ndim - 1)
                for r in order
            ],
            axis=-1,
        )

    def from_near(values, first, count):
        return jnp.concatenate(
            [
                lax.dynamic_slice_in_dim(
                    values, place[jnp.bitwise_xor(me, first + i)] * rows, rows, values.ndim - 1
                )
                for i in range(count)
            ],
            axis=-1,
        )

    def all_features(values):
        if tps == 2:
            pair = jnp.concatenate([values, swap(values, "tp", 2, 1)], axis=-1)
            half = shards // 2
            return to_near(pair, lambda o: jnp.bitwise_xor(o // half, tp) * half + o % half)
        return to_near(lax.all_gather(values, "tp", axis=1, tiled=True))

    def own_features(values):
        if tps == 2:
            half = shards // 2
            sent = swap(from_near(values, (1 - tp) * half, half).astype(BF16), "tp", 2, 1)
            return from_near(values, tp * half, half) + sent.astype(F32)
        whole = from_near(values, 0, shards).astype(BF16)
        return lax.psum_scatter(whole, "tp", scatter_dimension=1, tiled=True).astype(F32)

    def halves(left):
        count = left.shape[1] // 2
        return left[:, count:], swap(left[:, :count], "shard", shards, 1)

    def scatter_rows(left, right):
        peer = swap(right, "shard", shards, 1)
        parts = [
            dot_tn(left[0][:, at : at + rows], right) + dot_tn(left[1][:, at : at + rows], peer)
            for at in range(0, left[0].shape[1], rows)
        ]
        for bit in bits[1:]:
            count = len(parts) // 2
            moved = [swap(part.astype(BF16), "shard", shards, bit) for part in parts[:count]]
            parts = [part + other.astype(F32) for part, other in zip(parts[count:], moved)]
        return parts[0]

    def finish_rows(near):
        count = rows // ctxs
        piece = lambda p: lax.dynamic_slice_in_dim(near, jnp.clip(p, 0, ctxs - 1) * count, count, 0)
        from_left, from_right = None, None
        for step in range(1, ctxs):
            up, down = piece(ctxs - step + ctx), piece(step + ctx - ctxs)
            if step > 1:
                up, down = up + from_left.astype(F32), down + from_right.astype(F32)
            from_left = lax.ppermute(up.astype(BF16), "ctx", [(i, i + 1) for i in range(min(step, ctxs - 1))])
            from_right = lax.ppermute(
                down.astype(BF16), "ctx", [(i, i - 1) for i in range(max(ctxs - step, 1), ctxs)]
            )
        own = (piece(ctx) + from_left.astype(F32) + from_right.astype(F32)).astype(BF16)
        lower, upper = [own], [own]
        for _ in range(1, ctxs):
            lower.append(lax.ppermute(lower[-1], "ctx", [(i, i + 1) for i in range(ctxs - 1)]))
            upper.append(lax.ppermute(upper[-1], "ctx", [(i + 1, i) for i in range(ctxs - 1)]))
        line = jnp.concatenate(lower[:0:-1] + upper, axis=0)
        return lax.dynamic_slice_in_dim(line, (ctxs - 1 - ctx) * count, rows, 0)

    x_near = all_features(block_input.reshape(tokens, width_part))
    cot_near = all_features(out_cotangent.reshape(tokens, width_part))
    qkv_low = qkv_weight.astype(BF16)
    kv_full = [
        gather_rows(qkv_low[:, c * per : (c + 1) * per, HD:].reshape(rows, per * 2 * HD))
        for c in range(chunks)
    ]
    q_full = gather_rows(qkv_low[:, :, :HD].reshape(rows, heads * HD))
    widen_full = gather_rows(widen_weight.astype(BF16))
    dense_full = gather_rows(dense_weight.astype(BF16))
    narrow_full = gather_rows(narrow_weight.astype(BF16))
    gains = to_near(norm_gains)
    shifts = to_near(norm_shifts)

    inputs_wide = x_near.astype(F32)
    row_mean = jnp.mean(inputs_wide, axis=-1, keepdims=True)
    centered = inputs_wide - row_mean
    inv_std = lax.rsqrt(jnp.mean(centered * centered, axis=-1, keepdims=True) + norm_eps)
    normed = centered * inv_std
    first_in = (normed * gains[0] + shifts[0]).astype(BF16)
    second_in = (normed * gains[1] + shifts[1]).astype(BF16)

    cot_halves, first_halves, second_halves = halves(cot_near), halves(first_in), halves(second_in)

    segs = segment_ids.reshape(full_len)
    here = lax.dynamic_slice_in_dim(segs, ctx * tokens, tokens, 0)
    doc_start = jnp.zeros((tokens,), jnp.int32)
    for doc in range(DOC_IDS - 1):
        doc_start = doc_start + jnp.where(here > doc, jnp.sum((segs == doc).astype(jnp.int32)), 0)
    query_index = ctx * tokens + jnp.arange(tokens, dtype=jnp.int32)
    positions = (query_index - doc_start).astype(F32)[:, None]
    inv_freq = 10000.0 ** (-2.0 * jnp.arange(ROT // 2, dtype=F32) / ROT)
    angles = positions * inv_freq
    cos_table = jnp.concatenate([jnp.cos(angles), jnp.cos(angles)], -1)
    sin_table = jnp.concatenate([jnp.sin(angles), jnp.sin(angles)], -1)
    starts = (doc_start - (ctx - back) * tokens).reshape(1, tokens)
    low = starts[0, ::Q_TILE] // K_TILE

    head_bias = lax.dynamic_slice_in_dim(attn_bias, tp * heads, heads, 0)
    windows = []
    for c in range(chunks):
        bias = head_bias[c * per : (c + 1) * per, HD:].reshape(-1)
        kv = dot_nn(first_in, kv_full[c]) + bias
        kv = rotate_wide(kv, cos_table, sin_table, 2 * HD).astype(BF16)
        held = [kv]
        for _ in range(back):
            held.insert(0, lax.ppermute(held[0], "ctx", [(i, i + 1) for i in range(ctxs - 1)]))
        windows.append(held)
    q_bias = head_bias[:, :HD].reshape(-1)
    query = rotate_wide(dot_nn(first_in, q_full) + q_bias, cos_table, sin_table, HD)
    query = (query.astype(BF16) * (HD ** (-0.5))).astype(BF16)
    attended_grad = dot_nn(cot_near, dense_full).astype(BF16)

    hidden_slice = lax.dynamic_slice_in_dim(hidden_bias, tp * hidden, hidden, 0)
    widened = dot_nn(second_in, widen_full) + hidden_slice
    activated, gelu_back = jax.vjp(lambda u: jax.nn.gelu(u, approximate=False), widened)
    activated = activated.astype(BF16)
    narrow_near = scatter_rows(cot_halves, activated)
    widened_grad = gelu_back(dot_nn(cot_near, narrow_full))[0].astype(BF16)
    widen_near = scatter_rows(second_halves, widened_grad)
    second_grad = dot_nt(widened_grad, widen_full)

    attended, query_grads, kv_grads = [], [], []
    for c in range(chunks):
        span = slice(c * per * HD, (c + 1) * per * HD)
        out, dq, *dkv = attention(
            query[:, span], attended_grad[:, span], windows[c], starts, low
        )
        attended.append(out)
        query_grads.append(dq)
        total = dkv[0]
        for b in range(back):
            moved = lax.ppermute(
                total.astype(BF16), "ctx", [(i + 1, i) for i in range(ctxs - 1)]
            )
            total = dkv[b + 1] + moved.astype(F32)
        kv_grads.append(rotate_wide(total, cos_table, -sin_table, 2 * HD).astype(BF16))
    attended = jnp.concatenate(attended, axis=-1)
    query_grad = rotate_wide(
        jnp.concatenate(query_grads, axis=-1), cos_table, -sin_table, HD
    ).astype(BF16)

    dense_near = scatter_rows(cot_halves, attended)
    branch = dot_nt(attended, dense_full) + dot_nt(activated, narrow_full)
    branch_own = own_features(branch)
    bias_part = lax.dynamic_slice_in_dim(out_bias, tp * width_part, width_part, 1)
    block_out = (
        block_input.reshape(tokens, width_part).astype(F32)
        + branch_own
        + bias_part[0]
        + bias_part[1]
    ).astype(BF16)

    q_near = scatter_rows(first_halves, query_grad)
    kv_near = [scatter_rows(first_halves, kv_grads[c]) for c in range(chunks)]
    first_grad = dot_nt(query_grad, q_full)
    for c in range(chunks):
        first_grad = first_grad + dot_nt(kv_grads[c], kv_full[c])

    combined = first_grad * gains[0] + second_grad * gains[1]
    stats = jnp.stack([jnp.sum(combined, axis=-1), jnp.sum(combined * normed, axis=-1)])
    stats = all_sum(stats, "tp", tps) / D
    own_combined = own_features(combined)
    own_normed = (block_input.reshape(tokens, width_part).astype(F32) - row_mean) * inv_std
    cot_own = out_cotangent.reshape(tokens, width_part).astype(F32)
    input_grad = cot_own + inv_std * (
        own_combined - stats[0][:, None] - own_normed * stats[1][:, None]
    )
    input_grad = input_grad.astype(BF16)

    def add_up(parts):
        flat = jnp.concatenate([part.reshape(-1) for part in parts])
        for axis in ("shard", "ctx", "tp"):
            flat = all_sum(flat, axis, sizes[axis])
        found, at = [], 0
        for part in parts:
            found.append(flat[at : at + part.size].reshape(part.shape))
            at += part.size
        return found

    def spread_tp(part, count):
        zero = jnp.zeros((count,), F32)
        return lax.dynamic_update_slice_in_dim(zero, part, tp * (count // tps), 0)

    back_order = lambda rows_of: from_near(rows_of, 0, shards)
    hidden_sum, second_gain, second_shift, out_sum = add_up(
        [
            spread_tp(jnp.sum(widened_grad.astype(F32), axis=0), FF),
            back_order(jnp.sum(second_grad * normed, axis=0)),
            back_order(jnp.sum(second_grad, axis=0)),
            spread_tp(jnp.sum(cot_own, axis=0), D),
        ]
    )
    bias_rows = jnp.concatenate(
        [jnp.sum(query_grad.astype(F32), axis=0).reshape(heads, HD)]
        + [
            jnp.concatenate(
                [
                    jnp.sum(kv_grads[c].astype(F32), axis=0).reshape(per, 2 * HD)
                    for c in range(chunks)
                ],
                axis=0,
            )
        ],
        axis=-1,
    )
    attn_sum, first_gain, first_shift = add_up(
        [
            spread_tp(bias_rows.reshape(-1), H * 3 * HD),
            back_order(jnp.sum(first_grad * normed, axis=0)),
            back_order(jnp.sum(first_grad, axis=0)),
        ]
    )
    hidden_bias_grad = hidden_sum
    out_bias_grad = jnp.stack([out_sum, out_sum])
    attn_bias_grad = attn_sum.reshape(H, 3 * HD)
    gains_grad = jnp.stack([first_gain, second_gain])
    shifts_grad = jnp.stack([first_shift, second_shift])

    narrow_grad = finish_rows(narrow_near).astype(F32)
    widen_grad = finish_rows(widen_near).astype(F32)
    dense_grad = finish_rows(dense_near).astype(F32)
    q_rows = finish_rows(q_near).reshape(rows, heads, HD)
    kv_rows = [finish_rows(near).reshape(rows, per, 2 * HD) for near in kv_near]
    qkv_grad = jnp.concatenate([q_rows, jnp.concatenate(kv_rows, axis=1)], axis=-1).astype(F32)

    qkv_new = adam_step(
        qkv_weight, qkv_grad, qkv_weight_first, qkv_weight_second, matrix_rate, decay_rate
    )
    dense_new = adam_step(
        dense_weight, dense_grad, dense_weight_first, dense_weight_second, matrix_rate, decay_rate
    )
    widen_new = adam_step(
        widen_weight, widen_grad, widen_weight_first, widen_weight_second, matrix_rate, decay_rate
    )
    narrow_new = adam_step(
        narrow_weight,
        narrow_grad,
        narrow_weight_first,
        narrow_weight_second,
        matrix_rate,
        decay_rate,
    )
    attn_new = adam_step(
        attn_bias, attn_bias_grad, attn_bias_first, attn_bias_second, vector_rate, 0.0
    )
    hidden_new = adam_step(
        hidden_bias, hidden_bias_grad, hidden_bias_first, hidden_bias_second, vector_rate, 0.0
    )
    out_new = adam_step(out_bias, out_bias_grad, out_bias_first, out_bias_second, vector_rate, 0.0)
    gains_new = adam_step(
        norm_gains, gains_grad, norm_gains_first, norm_gains_second, vector_rate, 0.0
    )
    shifts_new = adam_step(
        norm_shifts, shifts_grad, norm_shifts_first, norm_shifts_second, vector_rate, 0.0
    )
    return (
        block_out[None],
        input_grad[None],
        qkv_grad,
        qkv_new[0],
        qkv_new[1],
        qkv_new[2],
        dense_grad,
        dense_new[0],
        dense_new[1],
        dense_new[2],
        widen_grad,
        widen_new[0],
        widen_new[1],
        widen_new[2],
        narrow_grad,
        narrow_new[0],
        narrow_new[1],
        narrow_new[2],
        attn_bias_grad,
        attn_new[0],
        attn_new[1],
        attn_new[2],
        hidden_bias_grad,
        hidden_new[0],
        hidden_new[1],
        hidden_new[2],
        out_bias_grad,
        out_new[0],
        out_new[1],
        out_new[2],
        gains_grad,
        gains_new[0],
        gains_new[1],
        gains_new[2],
        shifts_grad,
        shifts_new[0],
        shifts_new[1],
        shifts_new[2],
    )


def solution(mesh):
    placed = (
        P("shard", "ctx", "tp"),
        P("shard", "ctx", "tp"),
        P("shard", None),
        P("shard", "tp", None),
        P("shard", "tp", None),
        P("shard", "tp", None),
        P("shard", "tp"),
        P("shard", "tp"),
        P("shard", "tp"),
        P("shard", "tp"),
        P("shard", "tp"),
        P("shard", "tp"),
        P("shard", "tp"),
        P("shard", "tp"),
        P("shard", "tp"),
        P(),
        P(),
        P(),
        P(),
        P(),
        P(),
        P(),
        P(),
        P(),
        P(),
        P(),
        P(),
        P(),
        P(),
        P(),
    )
    return jax.shard_map(
        functools.partial(body, dict(mesh.shape)),
        mesh=mesh,
        in_specs=placed,
        out_specs=(
            P("shard", "ctx", "tp"),
            P("shard", "ctx", "tp"),
            P("shard", "tp", None),
            P("shard", "tp", None),
            P("shard", "tp", None),
            P("shard", "tp", None),
            P("shard", "tp"),
            P("shard", "tp"),
            P("shard", "tp"),
            P("shard", "tp"),
            P("shard", "tp"),
            P("shard", "tp"),
            P("shard", "tp"),
            P("shard", "tp"),
            P("shard", "tp"),
            P("shard", "tp"),
            P("shard", "tp"),
            P("shard", "tp"),
            P(),
            P(),
            P(),
            P(),
            P(),
            P(),
            P(),
            P(),
            P(),
            P(),
            P(),
            P(),
            P(),
            P(),
            P(),
            P(),
            P(),
            P(),
            P(),
            P(),
        ),
        check_vma=False,
    )
```
